256 devices in a mesh: tm: 16 (over y, x_lo, core), space: 16 (over x_hi, z).
Axes of the slice: x: 4 (x_hi: 2, x_lo: 2; x = x_hi * 2 + x_lo), y: 4, z: 8, core: 2. Of those that a mesh axis runs over, the one named last changes fastest.
Arguments:
- eigvec: bfloat16 [16, 2, 3, 16384, 384], P('tm', None, None, 'space'), may hold values from -1 to 1
- momenta: int32 [2, 3], replicated, may hold values from -2 to 2
- peram: bfloat16 [16, 2, 384, 4, 384], P('tm', None, 'space'), may hold values from -0.0078125 to 0.0078125
Outputs:
- dressed: bfloat16 [16, 384, 4, 2, 384], P('tm', 'space')
The draws below stay inside these ranges and needn't reach their ends.
All inputs are finite; a program needn't handle non-finite values.
Results may differ from the reference program's by a relative error of at most 0.0073.
Values may be sent and summed in bfloat16 or wider, within the bound.
No kernel may reach another device: no remote copies, remote signals or barrier semaphores. Data moves between devices by JAX's collectives and lax.ppermute only.
A program may use at most 128 MiB of HBM per device.

```python
import math
import jax
import jax.numpy as jnp
from jax import lax

NVEC = 384
SPIN = 4
COLORS = 3
LAT = 32
NMOM = 2
VOL = 16384
NT = 16


def place_ends(entries, stream_key, low, high):
    longest = entries.shape.index(max(entries.shape))
    spots = []
    for shift in (0, 1):
        where = [jax.random.randint(jax.random.fold_in(stream_key, axis), (), 0, length) for axis, length in enumerate(entries.shape)]
        where[longest] = (where[longest] + shift) % entries.shape[longest]
        spots.append(tuple(where))
    return entries.at[spots[0]].set(low).at[spots[1]].set(high)


def block_scale(stream_key, shape, split, smallest, high):
    def one(dim, blocks):
        draws = jax.random.uniform(jax.random.fold_in(jax.random.fold_in(stream_key, 6), dim), (blocks,), jnp.float32, smallest / len(split), high / len(split))
        return jnp.repeat(jnp.exp(draws), shape[dim] // blocks).reshape((-1,) + (1,) * (len(shape) - dim - 1))

    gain = one(*split[0])
    for cut in split[1:]:
        gain = gain * one(*cut)
    return gain


def gaussian(key, shape, width, bound, shards=(), kind=jnp.bfloat16):
    loudness = block_scale(key, shape, shards, -0.22, 0.18) if shards else 1.0
    drawn = jax.random.normal(key, shape, jnp.float32) * width * loudness
    return jnp.minimum(jnp.maximum(drawn, -bound), bound).astype(kind)


def setup_inputs(seed: int = 0) -> dict:
    key_list = jax.random.split(jax.random.key(seed), 4)
    return {
        "eigvec": gaussian(key_list[0], (NT, 2, COLORS, VOL, NVEC), ((3 * VOL) ** -0.25), 1.0, ((0, 16), (3, 16))),
        "momenta": place_ends(jax.random.randint(key_list[1], (NMOM, 3), -2, 3), jax.random.fold_in(key_list[1], 1), -2, 2).astype(jnp.int32),
        "peram": gaussian(key_list[2], (NT, 2, NVEC, SPIN, NVEC), (0.2 * NVEC ** -1), 0.0078125, ((0, 16), (2, 16))),
    }


def phase_gram(vectors, momentum):
    sites = jnp.arange(VOL, dtype=jnp.int32)
    coord_x = sites % LAT
    coord_y = (sites // LAT) % LAT
    coord_z = sites // (LAT * LAT)
    winding = jnp.mod(momentum[0] * coord_x + momentum[1] * coord_y + momentum[2] * coord_z, LAT)
    theta = winding.astype(jnp.float32) * (2.0 * math.pi / LAT)
    cosine = jnp.cos(theta)[None, :, None]
    sine = jnp.sin(theta)[None, :, None]
    real_part = vectors[0].astype(jnp.float32)
    imag_part = vectors[1].astype(jnp.float32)
    phased_re = (cosine * real_part + sine * imag_part).astype(jnp.bfloat16)
    phased_im = (cosine * imag_part - sine * real_part).astype(jnp.bfloat16)
    upper = jnp.concatenate([phased_re, phased_im], axis=-1)
    lower = jnp.concatenate([phased_im, -phased_re], axis=-1)
    right = jnp.stack([upper, lower]).reshape(2 * COLORS * VOL, 2 * NVEC)
    left = vectors.reshape(2 * COLORS * VOL, NVEC)
    gram = lax.dot_general(left, right, (((0,), (0,)), ((), ())), preferred_element_type=jnp.float32)
    return gram.astype(jnp.bfloat16)


def apply_pair(operands):
    sink, source, tau = operands
    sink_re = sink[:, :NVEC]
    sink_im = sink[:, NVEC:]
    left = jnp.stack([jnp.concatenate([sink_re, -sink_im], axis=1), jnp.concatenate([sink_im, sink_re], axis=1)], axis=1)
    left = left.reshape(2 * NVEC, 2 * NVEC)
    mixed = jnp.dot(left, tau.reshape(2 * NVEC, SPIN * NVEC), preferred_element_type=jnp.float32)
    mixed = mixed.astype(jnp.bfloat16).reshape(NVEC, 2, SPIN * NVEC)
    mixed_re = mixed[:, 0].reshape(NVEC * SPIN, NVEC)
    mixed_im = mixed[:, 1].reshape(NVEC * SPIN, NVEC)
    source_re = source[:, :NVEC]
    source_im = source[:, NVEC:]
    right = jnp.concatenate([source, jnp.concatenate([-source_im, source_re], axis=1)], axis=0)
    dressed = jnp.dot(jnp.concatenate([mixed_re, mixed_im], axis=1), right, preferred_element_type=jnp.float32)
    return dressed.reshape(NVEC, SPIN, 2, NVEC).astype(jnp.bfloat16)


def reference(eigvec, momenta, peram):
    def both(vectors):
        return jnp.stack([phase_gram(vectors, momenta[0]), phase_gram(vectors, momenta[1])])

    elemental = lax.map(both, eigvec)
    source = elemental[::-1, 1]
    return lax.map(apply_pair, (elemental[:, 0], source, peram))
```

```python
import functools, math
import jax, jax.numpy as jnp
from jax import lax
from jax.experimental import pallas as pl
from jax.experimental.pallas import tpu as pltpu
from jax.sharding import PartitionSpec as P

LAT=32
LANES=128


def phase_of(winding):
    octant = winding + 4
    quadrant = (octant >> 3) & 3
    angle = ((octant & 7) - 4).astype(jnp.float32) * (2.0 * math.pi / LAT)
    square = angle * angle
    sine = angle * (1 + square * (-1 / 6 + square * (1 / 120 + square * (-1 / 5040 + square * (1 / 362880)))))
    cosine = 1 + square * (-1 / 2 + square * (1 / 24 + square * (-1 / 720 + square * (1 / 40320 - square * (1 / 3628800)))))
    swap = (quadrant & 1) == 1
    cos_out = jnp.where(swap, sine, cosine)
    sin_out = jnp.where(swap, cosine, sine)
    cos_out = jnp.where((quadrant == 1) | (quadrant == 2), -cos_out, cos_out)
    sin_out = jnp.where(quadrant >= 2, -sin_out, sin_out)
    return cos_out, sin_out


def gram_kernel(which, split, momenta, vec_ref, *refs):
    left_ref, right_ref, acc_ref = refs[-3:]
    step = pl.program_id(0)
    _, _, colors, sites, nvec = vec_ref.shape
    space = lax.axis_index("space")
    half = space // 8
    row = lax.broadcasted_iota(jnp.int32, (sites, LANES), 0) + step * sites
    winding = momenta[which, 0] * (row & 31) + momenta[which, 1] * (row >> 5) + momenta[which, 2] * space
    cosine, sine = phase_of(winding & 31)
    cosine = jnp.concatenate([cosine] * (nvec // LANES), axis=1)
    sine = jnp.concatenate([sine] * (nvec // LANES), axis=1)
    for color in range(colors):
        re = vec_ref[0, 0, color]
        im = vec_ref[0, 1, color]
        re32 = re.astype(jnp.float32)
        im32 = im.astype(jnp.float32)
        at = pl.ds(color * sites, sites)
        right_ref[at, :nvec] = (cosine * re32 + sine * im32).astype(jnp.bfloat16)
        right_ref[at, nvec:] = (cosine * im32 - sine * re32).astype(jnp.bfloat16)
        left_ref[at, :nvec] = re
        left_ref[at, nvec:] = im
    part = lax.dot_general(left_ref[...], right_ref[...], (((0,), (0,)), ((), ())), preferred_element_type=jnp.float32)
    @pl.when(step == 0)
    def _():
        acc_ref[...] = part
    @pl.when(step > 0)
    def _():
        acc_ref[...] += part
    @pl.when(step == pl.num_programs(0) - 1)
    def _():
        def put(out_ref, start):
            rows = out_ref.shape[0]
            real = pl.ds(start, rows)
            imag = pl.ds(start + nvec, rows)
            out_ref[:, :nvec] = (acc_ref[real, :nvec] + acc_ref[imag, nvec:]).astype(out_ref.dtype)
            out_ref[:, nvec:] = (acc_ref[real, nvec:] - acc_ref[imag, :nvec]).astype(out_ref.dtype)

        if split:
            rows = nvec // 2
            put(refs[0], pl.multiple_of((1 - half) * rows, rows))
            put(refs[1], pl.multiple_of(half * rows, rows))
        else:
            put(refs[0], 0)


def gram(eigvec, momenta, which, split, chunk=256):
    _, _, colors, sites, nvec = eigvec.shape
    depth = colors * chunk
    if split:
        outs = [((nvec // 2, 2 * nvec), jnp.bfloat16), ((nvec // 2, 2 * nvec), jnp.float32)]
    else:
        outs = [((nvec, 2 * nvec), jnp.bfloat16)]
    return pl.pallas_call(
        functools.partial(gram_kernel, which, split),
        grid_spec=pltpu.PrefetchScalarGridSpec(
            num_scalar_prefetch=1,
            grid=(sites // chunk,),
            in_specs=[pl.BlockSpec((1, 2, colors, chunk, nvec), lambda i, m: (0, 0, 0, i, 0))],
            out_specs=[pl.BlockSpec(shape, lambda i, m: (0, 0)) for shape, _ in outs],
            scratch_shapes=[
                pltpu.VMEM((depth, 2 * nvec), jnp.bfloat16),
                pltpu.VMEM((depth, 2 * nvec), jnp.bfloat16),
                pltpu.VMEM((2 * nvec, 2 * nvec), jnp.float32),
            ],
        ),
        out_shape=[jax.ShapeDtypeStruct(shape, kind) for shape, kind in outs],
        compiler_params=pltpu.CompilerParams(
            dimension_semantics=("arbitrary",), vmem_limit_bytes=62 << 20
        ),
        cost_estimate=pl.CostEstimate(
            flops=8 * nvec * nvec * colors * sites, bytes_accessed=eigvec.size * 2, transcendentals=0
        ),
    )(momenta, eigvec)


Z_GROUPS = [list(range(8)), list(range(8, 16))]
SPIN = 4


def exchange(parts, groups=None):
    return lax.all_to_all(parts, "space", split_axis=0, concat_axis=0, tiled=True, axis_index_groups=groups)


def swap(value, bit):
    return lax.ppermute(value, "space", [(i, i ^ bit) for i in range(16)])


def total(parts):
    return parts.astype(jnp.float32).sum(axis=0).astype(jnp.bfloat16)


def steps(eigvec, momenta, peram):
    tau = peram[0]
    nrows, nvec = tau.shape[1], tau.shape[3]
    place = lax.axis_index("space")
    spins = jnp.broadcast_to(tau.transpose(2, 0, 1, 3).reshape(2, 1, 2, 2, nrows, nvec), (2, 4, 2, 2, nrows, nvec))
    tau = exchange(spins.reshape(16, 2, nrows, nvec))
    tau = tau.transpose(1, 0, 2, 3).reshape(2 * nvec, nvec)
    (source,) = gram(eigvec, momenta, 1, False)
    source = exchange(source.reshape(16, nrows, 2 * nvec))
    share = total(source)
    share = lax.ppermute(share, "tm", [(t, 15 - t) for t in range(16)])
    source = exchange(jnp.broadcast_to(share, (16, *share.shape)))
    send, keep = gram(eigvec, momenta, 0, True)
    arrived = swap(send, 8)
    pair = (keep + arrived.astype(jnp.float32)).astype(jnp.bfloat16)
    parts = exchange(pair.reshape(8, nrows, 2 * nvec), Z_GROUPS)
    rows = total(parts)[None]
    rows = jnp.concatenate([rows, swap(rows, 1)])
    rows = jnp.concatenate([rows, swap(rows, 8)])
    rows_re, rows_im = rows[..., :nvec], rows[..., nvec:]
    left = jnp.concatenate(
        [jnp.concatenate([rows_re, -rows_im], axis=-1), jnp.concatenate([rows_im, rows_re], axis=-1)], axis=1
    ).reshape(8 * nrows, 2 * nvec)
    mixed = jnp.dot(left, tau, preferred_element_type=jnp.float32).astype(jnp.bfloat16)
    mixed = mixed.reshape(2, 2, 2, nrows, nvec)
    mixed = jnp.stack([mixed[0], swap(mixed[1], 8)])
    mixed = jnp.stack([mixed[:, 0], swap(mixed[:, 1], 1)], axis=1)
    mixed = jnp.where(place % 2 == 1, mixed[:, ::-1], mixed)
    mixed = jnp.where(place // 8 == 1, mixed[::-1], mixed)
    mixed = mixed.transpose(3, 0, 1, 2, 4).reshape(nrows * SPIN, 2 * nvec)
    source = source.reshape(nvec, 2 * nvec)
    source_re, source_im = source[:, :nvec], source[:, nvec:]
    right = jnp.concatenate([source, jnp.concatenate([-source_im, source_re], axis=1)], axis=0)
    dressed = jnp.dot(mixed, right, preferred_element_type=jnp.float32)
    return dressed.reshape(1, nrows, SPIN, 2, nvec).astype(jnp.bfloat16)


def solution(mesh):
    return jax.shard_map(
        steps,
        mesh=mesh,
        in_specs=(P("tm", None, None, "space", None), P(), P("tm", None, "space", None, None)),
        out_specs=P("tm", "space", None, None, None),
        check_vma=False,
    )
```

```python
import functools, math
import jax, jax.numpy as jnp
from jax import lax
from jax.experimental import pallas as pl
from jax.experimental.pallas import tpu as pltpu
from jax.sharding import PartitionSpec as P

LAT=32
LANES = 128
MEMBER_BITS = (0, 1, 8, 9)
QUAD_BITS = (0, 2, 4, 6)


def phase_of(winding):
    octant = winding + 4
    quadrant = (octant >> 3) & 3
    angle = ((octant & 7) - 4).astype(jnp.float32) * (2.0 * math.pi / LAT)
    square = angle * angle
    sine = angle * (1 + square * (-1 / 6 + square * (1 / 120 + square * (-1 / 5040 + square * (1 / 362880)))))
    cosine = 1 + square * (-1 / 2 + square * (1 / 24 + square * (-1 / 720 + square * (1 / 40320 - square * (1 / 3628800)))))
    swap = (quadrant & 1) == 1
    cos_out = jnp.where(swap, sine, cosine)
    sin_out = jnp.where(swap, cosine, sine)
    cos_out = jnp.where((quadrant == 1) | (quadrant == 2), -cos_out, cos_out)
    sin_out = jnp.where(quadrant >= 2, -sin_out, sin_out)
    return cos_out, sin_out


def gram_kernel(which, momenta, vec_ref, keep_ref, *refs):
    send_refs = refs[:3]
    left_ref, right_ref, acc_ref = refs[3:]
    step = pl.program_id(0)
    _, _, colors, sites, nvec = vec_ref.shape
    space = lax.axis_index("space")
    row = lax.broadcasted_iota(jnp.int32, (sites, LANES), 0) + step * sites
    winding = momenta[which, 0] * (row & 31) + momenta[which, 1] * (row >> 5) + momenta[which, 2] * space
    cosine, sine = phase_of(winding & 31)
    cosine = jnp.concatenate([cosine] * (nvec // LANES), axis=1)
    sine = jnp.concatenate([sine] * (nvec // LANES), axis=1)
    for color in range(colors):
        re = vec_ref[0, 0, color]
        im = vec_ref[0, 1, color]
        re32 = re.astype(jnp.float32)
        im32 = im.astype(jnp.float32)
        at = pl.ds(color * sites, sites)
        right_ref[at, :nvec] = (cosine * re32 + sine * im32).astype(jnp.bfloat16)
        right_ref[at, nvec:] = (cosine * im32 - sine * re32).astype(jnp.bfloat16)
        left_ref[at, :nvec] = re
        left_ref[at, nvec:] = im
    part = lax.dot_general(
        left_ref[...], right_ref[...], (((0,), (0,)), ((), ())), preferred_element_type=jnp.float32
    )

    @pl.when(step == 0)
    def _():
        acc_ref[...] = part

    @pl.when(step > 0)
    def _():
        acc_ref[...] += part

    @pl.when(step == pl.num_programs(0) - 1)
    def _():
        rows = nvec // 16
        for member, out_ref in enumerate((keep_ref, *send_refs)):
            target = space ^ MEMBER_BITS[member]
            for quad in range(4):
                owner = (target & 9) | (2 * quad)
                start = pl.multiple_of(owner * rows, 8)
                real = pl.ds(start, rows)
                imag = pl.ds(pl.multiple_of(start + nvec, 8), rows)
                at = pl.ds(quad * rows, rows)
                out_ref[at, :nvec] = (acc_ref[real, :nvec] + acc_ref[imag, nvec:]).astype(out_ref.dtype)
                out_ref[at, nvec:] = (acc_ref[real, nvec:] - acc_ref[imag, :nvec]).astype(out_ref.dtype)


def gram(eigvec, momenta, which, chunk=256):
    _, _, colors, sites, nvec = eigvec.shape
    depth = colors * chunk
    shape = (nvec // 4, 2 * nvec)
    kinds = [jnp.float32] + [jnp.bfloat16] * 3
    return pl.pallas_call(
        functools.partial(gram_kernel, which),
        grid_spec=pltpu.PrefetchScalarGridSpec(
            num_scalar_prefetch=1,
            grid=(sites // chunk,),
            in_specs=[pl.BlockSpec((1, 2, colors, chunk, nvec), lambda i, m: (0, 0, 0, i, 0))],
            out_specs=[pl.BlockSpec(shape, lambda i, m: (0, 0)) for _ in kinds],
            scratch_shapes=[
                pltpu.VMEM((depth, 2 * nvec), jnp.bfloat16),
                pltpu.VMEM((depth, 2 * nvec), jnp.bfloat16),
                pltpu.VMEM((2 * nvec, 2 * nvec), jnp.float32),
            ],
        ),
        out_shape=[jax.ShapeDtypeStruct(shape, kind) for kind in kinds],
        compiler_params=pltpu.CompilerParams(
            dimension_semantics=("arbitrary",), vmem_limit_bytes=62 << 20
        ),
        cost_estimate=pl.CostEstimate(
            flops=8 * nvec * nvec * colors * sites, bytes_accessed=eigvec.size * 2, transcendentals=0
        ),
    )(momenta, eigvec)


SPIN = 4


def exchange(parts):
    return lax.all_to_all(parts, "space", split_axis=0, concat_axis=0, tiled=True)


def swap(value, bits):
    return lax.ppermute(value, "space", [(i, i ^ bits) for i in range(16)])


def reduce_rows(parts):
    keep = parts[0]
    rows = keep.shape[0] // 4
    arrived = [swap(parts[m], MEMBER_BITS[m]) for m in (1, 2, 3)]
    for value in arrived:
        keep = keep + value.astype(jnp.float32)
    keep = keep.reshape(4, rows, keep.shape[1])
    quad = lax.axis_index("space") // 2 % 4
    parts = [lax.dynamic_index_in_dim(keep, quad ^ m, keepdims=False) for m in range(4)]
    sends = [part.astype(jnp.bfloat16) for part in parts[1:]]
    arrived = [swap(sends[m - 1], QUAD_BITS[m]) for m in (1, 2, 3)]
    out = parts[0]
    for value in arrived:
        out = out + value.astype(jnp.float32)
    return out.astype(jnp.bfloat16)


def steps(eigvec, momenta, peram):
    tau = peram[0]
    nrows, nvec = tau.shape[1], tau.shape[3]
    place = lax.axis_index("space")
    spins = jnp.broadcast_to(tau.transpose(2, 0, 1, 3).reshape(2, 1, 2, 2, nrows, nvec), (2, 4, 2, 2, nrows, nvec))
    tau = exchange(spins.reshape(16, 2, nrows, nvec))
    tau = tau.transpose(1, 0, 2, 3).reshape(2 * nvec, nvec)
    source = gram(eigvec, momenta, 1)
    sink = gram(eigvec, momenta, 0)
    share = reduce_rows(source)
    share = lax.ppermute(share, "tm", [(t, 15 - t) for t in range(16)])
    source = exchange(jnp.broadcast_to(share, (16, *share.shape)))
    rows = reduce_rows(sink)
    rows = jnp.stack([rows] + [swap(rows, MEMBER_BITS[m]) for m in (1, 2, 3)])
    rows_re, rows_im = rows[..., :nvec], rows[..., nvec:]
    left = jnp.concatenate(
        [jnp.concatenate([rows_re, -rows_im], axis=-1), jnp.concatenate([rows_im, rows_re], axis=-1)], axis=1
    ).reshape(8 * nrows, 2 * nvec)
    mixed = jnp.dot(left, tau, preferred_element_type=jnp.float32).astype(jnp.bfloat16)
    mixed = mixed.reshape(4, 2, nrows, nvec)
    mixed = jnp.stack([mixed[0]] + [swap(mixed[m], MEMBER_BITS[m]) for m in (1, 2, 3)])
    mixed = mixed.reshape(2, 2, 2, nrows, nvec)
    mixed = jnp.where(place % 2 == 1, mixed[:, ::-1], mixed)
    mixed = jnp.where(place // 8 == 1, mixed[::-1], mixed)
    mixed = mixed.transpose(3, 0, 1, 2, 4).reshape(nrows * SPIN, 2 * nvec)
    source = source.reshape(nvec, 2 * nvec)
    source_re, source_im = source[:, :nvec], source[:, nvec:]
    right = jnp.concatenate([source, jnp.concatenate([-source_im, source_re], axis=1)], axis=0)
    dressed = jnp.dot(mixed, right, preferred_element_type=jnp.float32)
    return dressed.reshape(1, nrows, SPIN, 2, nvec).astype(jnp.bfloat16)


def solution(mesh):
    return jax.shard_map(
        steps,
        mesh=mesh,
        in_specs=(P("tm", None, None, "space", None), P(), P("tm", None, "space", None, None)),
        out_specs=P("tm", "space", None, None, None),
        check_vma=False,
    )
```

```python
import functools, math
import jax, jax.numpy as jnp
from jax import lax
from jax.experimental import pallas as pl
from jax.experimental.pallas import tpu as pltpu
from jax.sharding import PartitionSpec as P

LAT=32
LANES = 128
MEMBER_BITS = (0, 1, 8, 9)
QUAD_BITS = (0, 2, 4, 6)
QUAD_GROUPS = [[8 * h + 2 * q + lo for q in range(4)] for h in (0, 1) for lo in (0, 1)]


def phase_of(winding):
    octant = winding + 4
    quadrant = (octant >> 3) & 3
    angle = ((octant & 7) - 4).astype(jnp.float32) * (2.0 * math.pi / LAT)
    square = angle * angle
    sine = angle * (1 + square * (-1 / 6 + square * (1 / 120 + square * (-1 / 5040 + square * (1 / 362880)))))
    cosine = 1 + square * (-1 / 2 + square * (1 / 24 + square * (-1 / 720 + square * (1 / 40320 - square * (1 / 3628800)))))
    swap = (quadrant & 1) == 1
    cos_out = jnp.where(swap, sine, cosine)
    sin_out = jnp.where(swap, cosine, sine)
    cos_out = jnp.where((quadrant == 1) | (quadrant == 2), -cos_out, cos_out)
    sin_out = jnp.where(quadrant >= 2, -sin_out, sin_out)
    return cos_out, sin_out


def gram_kernel(which, momenta, vec_ref, keep_ref, *refs):
    send_refs = refs[:3]
    left_ref, right_ref, acc_ref = refs[3:]
    step = pl.program_id(0)
    _, _, colors, sites, nvec = vec_ref.shape
    space = lax.axis_index("space")
    row = lax.broadcasted_iota(jnp.int32, (sites, LANES), 0) + step * sites
    winding = momenta[which, 0] * (row & 31) + momenta[which, 1] * (row >> 5) + momenta[which, 2] * space
    cosine, sine = phase_of(winding & 31)
    cosine = jnp.concatenate([cosine] * (nvec // LANES), axis=1)
    sine = jnp.concatenate([sine] * (nvec // LANES), axis=1)
    for color in range(colors):
        re = vec_ref[0, 0, color]
        im = vec_ref[0, 1, color]
        re32 = re.astype(jnp.float32)
        im32 = im.astype(jnp.float32)
        at = pl.ds(color * sites, sites)
        right_ref[at, :nvec] = (cosine * re32 + sine * im32).astype(jnp.bfloat16)
        right_ref[at, nvec:] = (cosine * im32 - sine * re32).astype(jnp.bfloat16)
        left_ref[at, :nvec] = re
        left_ref[at, nvec:] = im
    part = lax.dot_general(
        left_ref[...], right_ref[...], (((0,), (0,)), ((), ())), preferred_element_type=jnp.float32
    )

    @pl.when(step == 0)
    def _():
        acc_ref[...] = part

    @pl.when(step > 0)
    def _():
        acc_ref[...] += part

    @pl.when(step == pl.num_programs(0) - 1)
    def _():
        rows = nvec // 16
        for member, out_ref in enumerate((keep_ref, *send_refs)):
            target = space ^ MEMBER_BITS[member]
            for quad in range(4):
                owner = (target & 9) | (2 * quad)
                start = pl.multiple_of(owner * rows, 8)
                real = pl.ds(start, rows)
                imag = pl.ds(pl.multiple_of(start + nvec, 8), rows)
                at = pl.ds(quad * rows, rows)
                out_ref[at, :nvec] = (acc_ref[real, :nvec] + acc_ref[imag, nvec:]).astype(out_ref.dtype)
                out_ref[at, nvec:] = (acc_ref[real, nvec:] - acc_ref[imag, :nvec]).astype(out_ref.dtype)


def gram(eigvec, momenta, which, chunk=256):
    _, _, colors, sites, nvec = eigvec.shape
    depth = colors * chunk
    shape = (nvec // 4, 2 * nvec)
    kinds = [jnp.float32] + [jnp.bfloat16] * 3
    return pl.pallas_call(
        functools.partial(gram_kernel, which),
        grid_spec=pltpu.PrefetchScalarGridSpec(
            num_scalar_prefetch=1,
            grid=(sites // chunk,),
            in_specs=[pl.BlockSpec((1, 2, colors, chunk, nvec), lambda i, m: (0, 0, 0, i, 0))],
            out_specs=[pl.BlockSpec(shape, lambda i, m: (0, 0)) for _ in kinds],
            scratch_shapes=[
                pltpu.VMEM((depth, 2 * nvec), jnp.bfloat16),
                pltpu.VMEM((depth, 2 * nvec), jnp.bfloat16),
                pltpu.VMEM((2 * nvec, 2 * nvec), jnp.float32),
            ],
        ),
        out_shape=[jax.ShapeDtypeStruct(shape, kind) for kind in kinds],
        compiler_params=pltpu.CompilerParams(
            dimension_semantics=("arbitrary",), vmem_limit_bytes=62 << 20
        ),
        cost_estimate=pl.CostEstimate(
            flops=8 * nvec * nvec * colors * sites, bytes_accessed=eigvec.size * 2, transcendentals=0
        ),
    )(momenta, eigvec)


SPIN = 4


def swap(value, bits):
    return lax.ppermute(value, "space", [(i, i ^ bits) for i in range(16)])


def around(parts, bits):
    return [parts[0]] + [swap(parts[m], bits[m]) for m in (1, 2, 3)]


def wide_sum(parts):
    out = parts[0]
    for value in parts[1:]:
        out = out + value.astype(jnp.float32)
    return out


def in_place(parts, here):
    parts = jnp.stack(parts)
    return jnp.stack([lax.dynamic_index_in_dim(parts, m ^ here, keepdims=False) for m in range(4)])


def spread(total, here):
    rows = total.shape[0] // 4
    total = total.reshape(4, rows, total.shape[1])
    parts = [lax.dynamic_index_in_dim(total, here ^ m, keepdims=False) for m in range(4)]
    return parts[:1] + [part.astype(jnp.bfloat16) for part in parts[1:]]


def steps(eigvec, momenta, peram):
    tau = peram[0]
    nrows, nvec = tau.shape[1], tau.shape[3]
    place = lax.axis_index("space")
    quad = place // 2 % 4
    member = place // 8 * 2 + place % 2
    tau = tau.transpose(2, 1, 0, 3).reshape(SPIN, nrows, 2 * nvec)
    spins = [lax.dynamic_index_in_dim(tau, member ^ m, keepdims=False) for m in range(4)]
    source = gram(eigvec, momenta, 1)
    sink = gram(eigvec, momenta, 0)
    first = around([source[0]] + [jnp.concatenate([source[m], spins[m]]) for m in (1, 2, 3)], MEMBER_BITS)
    source = wide_sum([first[0]] + [part[: 4 * nrows] for part in first[1:]])
    spins = in_place([spins[0]] + [part[4 * nrows :] for part in first[1:]], member)
    spins = lax.all_to_all(
        jnp.broadcast_to(spins, (4, *spins.shape)),
        "space",
        split_axis=0,
        concat_axis=0,
        tiled=True,
        axis_index_groups=QUAD_GROUPS,
    )
    tau = spins.reshape(4, 2, 2, nrows, 2, nvec).transpose(4, 1, 0, 2, 3, 5).reshape(2 * nvec, nvec)
    sink = wide_sum(around(sink, MEMBER_BITS))
    source = wide_sum(around(spread(source, quad), QUAD_BITS)).astype(jnp.bfloat16)
    share = lax.ppermute(source, "tm", [(t, 15 - t) for t in range(16)])
    sink = spread(sink, quad)
    second = around([share] + [jnp.concatenate([share, sink[m]]) for m in (1, 2, 3)], QUAD_BITS)
    rows = wide_sum([sink[0]] + [part[nrows:] for part in second[1:]]).astype(jnp.bfloat16)
    share = in_place([second[0]] + [part[:nrows] for part in second[1:]], quad)
    third = jnp.concatenate([share.reshape(4 * nrows, 2 * nvec), rows])
    third = around([third] * 4, MEMBER_BITS)
    rows = jnp.stack([part[4 * nrows :] for part in third])
    source = in_place([part[: 4 * nrows] for part in third], member)
    source = source.reshape(2, 2, 4, nrows, 2 * nvec).transpose(0, 2, 1, 3, 4).reshape(nvec, 2 * nvec)
    rows_re, rows_im = rows[..., :nvec], rows[..., nvec:]
    left = jnp.concatenate(
        [jnp.concatenate([rows_re, -rows_im], axis=-1), jnp.concatenate([rows_im, rows_re], axis=-1)], axis=1
    ).reshape(8 * nrows, 2 * nvec)
    mixed = jnp.dot(left, tau, preferred_element_type=jnp.float32).astype(jnp.bfloat16)
    mixed = mixed.reshape(4, 2, nrows, nvec)
    mixed = in_place(around([mixed[m] for m in range(4)], MEMBER_BITS), member)
    mixed = mixed.transpose(2, 0, 1, 3).reshape(nrows * SPIN, 2 * nvec)
    source_re, source_im = source[:, :nvec], source[:, nvec:]
    right = jnp.concatenate([source, jnp.concatenate([-source_im, source_re], axis=1)], axis=0)
    dressed = jnp.dot(mixed, right, preferred_element_type=jnp.float32)
    return dressed.reshape(1, nrows, SPIN, 2, nvec).astype(jnp.bfloat16)


def solution(mesh):
    return jax.shard_map(
        steps,
        mesh=mesh,
        in_specs=(P("tm", None, None, "space", None), P(), P("tm", None, "space", None, None)),
        out_specs=P("tm", "space", None, None, None),
        check_vma=False,
    )
```

```python
import functools
import math

import jax
import jax.numpy as jnp
from jax import lax
from jax.experimental import pallas as pl
from jax.experimental.pallas import tpu as pltpu
from jax.sharding import PartitionSpec as P


LAT = 32
LANES = 128
SPIN = 4
MEMBER_BITS = (0, 1, 8, 9)
QUAD_BITS = (0, 2, 4, 6)


def phase_of(winding):
    octant = (winding & 31) + 4
    quadrant = (octant >> 3) & 3
    angle = ((octant & 7) - 4).astype(jnp.float32) * (2.0 * math.pi / LAT)
    square = angle * angle
    sine = angle * (1 + square * (-1 / 6 + square * (1 / 120 + square * (-1 / 5040 + square * (1 / 362880)))))
    cosine = 1 + square * (-1 / 2 + square * (1 / 24 + square * (-1 / 720 + square * (1 / 40320 - square * (1 / 3628800)))))
    swap = (quadrant & 1) == 1
    cos_out = jnp.where(swap, sine, cosine)
    sin_out = jnp.where(swap, cosine, sine)
    cos_out = jnp.where((quadrant == 1) | (quadrant == 2), -cos_out, cos_out)
    sin_out = jnp.where(quadrant >= 2, -sin_out, sin_out)
    return cos_out, sin_out


def gram_kernel(which, chunks, momenta, vec_ref, spin_ref, keep_ref, *refs):
    send_refs = refs[:3]
    vec_buf, y_ref, left0, left1, right0, right1, acc_ref, sems = refs[3:]
    left = (left0, left1)
    right = (right0, right1)
    _, _, colors, sites, nvec = vec_ref.shape
    depth = sites // chunks
    rows_y = depth // LAT

    def fetch(step):
        return pltpu.make_async_copy(
            vec_ref.at[0, :, :, pl.ds(step * depth, depth), :], vec_buf.at[step], sems.at[step])

    for step in range(chunks):
        fetch(step).start()
    space = lax.axis_index("space")
    index = lax.broadcasted_iota(jnp.int32, (LAT, LANES), 0)
    cos_x, sin_x = phase_of(momenta[which, 0] * index)
    cos_y, sin_y = phase_of(momenta[which, 1] * index + momenta[which, 2] * space)
    y_ref[0] = cos_y
    y_ref[1] = sin_y

    def prepare(step):
        fetch(step).wait()
        for y in range(rows_y):
            at_y = step * rows_y + y
            cos_row = jnp.broadcast_to(y_ref[0, at_y : at_y + 1], (LAT, LANES))
            sin_row = jnp.broadcast_to(y_ref[1, at_y : at_y + 1], (LAT, LANES))
            cosine = cos_x * cos_row - sin_x * sin_row
            sine = sin_x * cos_row + cos_x * sin_row
            cosine = jnp.concatenate([cosine] * (nvec // LANES), axis=1)
            sine = jnp.concatenate([sine] * (nvec // LANES), axis=1)
            for color in range(colors):
                re = vec_buf[step, 0, color, y * LAT : (y + 1) * LAT]
                im = vec_buf[step, 1, color, y * LAT : (y + 1) * LAT]
                re32 = re.astype(jnp.float32)
                im32 = im.astype(jnp.float32)
                at = pl.ds(color * depth + y * LAT, LAT)
                right[step % 2][at, :nvec] = (cosine * re32 + sine * im32).astype(jnp.bfloat16)
                right[step % 2][at, nvec:] = (cosine * im32 - sine * re32).astype(jnp.bfloat16)
                left[step % 2][at, :nvec] = re
                left[step % 2][at, nvec:] = im

    prepare(0)
    for step in range(chunks):
        if step + 1 < chunks:
            prepare(step + 1)
        part = lax.dot_general(left[step % 2][...], right[step % 2][...], (((0,), (0,)), ((), ())),
                               preferred_element_type=jnp.float32)
        if step == 0:
            acc_ref[...] = part
        else:
            acc_ref[...] += part
    rows = nvec // 16
    here = space // 8 * 2 + space % 2
    for member, out_ref in enumerate((keep_ref, *send_refs)):
        target = space ^ MEMBER_BITS[member]
        for quad in range(4):
            owner = (target & 9) | (2 * quad)
            start = pl.multiple_of(owner * rows, 8)
            real = pl.ds(start, rows)
            imag = pl.ds(pl.multiple_of(start + nvec, 8), rows)
            at = pl.ds(quad * rows, rows)
            out_ref[at, :nvec] = (acc_ref[real, :nvec] + acc_ref[imag, nvec:]).astype(out_ref.dtype)
            out_ref[at, nvec:] = (acc_ref[real, nvec:] - acc_ref[imag, :nvec]).astype(out_ref.dtype)
        if spin_ref is not None and member:
            out_ref[pl.ds(4 * rows, rows), :] = spin_ref[here ^ member]


def gram(eigvec, momenta, which, spins=None, chunks=4):
    _, _, colors, sites, nvec = eigvec.shape
    depth = sites // chunks
    rows = nvec // 4
    extra = 0 if spins is None else spins.shape[1]
    outs = [((rows, 2 * nvec), jnp.float32)] + [((rows + extra, 2 * nvec), jnp.bfloat16)] * 3
    vmem = pl.BlockSpec(memory_space=pltpu.VMEM)
    kern = functools.partial(gram_kernel, which, chunks)
    if spins is None:
        body = lambda m, v, *r: kern(m, v, None, *r)
        ins = ()
    else:
        body = kern
        ins = (spins,)
    operand = pltpu.VMEM((colors * depth, 2 * nvec), jnp.bfloat16)
    return pl.pallas_call(
        body,
        in_specs=[pl.BlockSpec(memory_space=pltpu.SMEM), pl.BlockSpec(memory_space=pl.ANY)] + [vmem] * len(ins),
        out_specs=[vmem] * 4,
        scratch_shapes=[
            pltpu.VMEM((chunks, 2, colors, depth, nvec), jnp.bfloat16),
            pltpu.VMEM((2, LAT, LANES), jnp.float32),
            operand, operand, operand, operand,
            pltpu.VMEM((2 * nvec, 2 * nvec), jnp.float32),
            pltpu.SemaphoreType.DMA((chunks,)),
        ],
        out_shape=[jax.ShapeDtypeStruct(shape, kind) for shape, kind in outs],
        compiler_params=pltpu.CompilerParams(vmem_limit_bytes=62 << 20),
        cost_estimate=pl.CostEstimate(flops=8 * nvec * nvec * colors * sites, bytes_accessed=eigvec.size * 2, transcendentals=0),
    )(momenta, eigvec, *ins)


def swap(value, bits):
    return lax.ppermute(value, "space", [(i, i ^ bits) for i in range(16)])


def around(parts, bits):
    return [parts[0]] + [swap(parts[m], bits[m]) for m in (1, 2, 3)]


def wide_sum(parts):
    out = parts[0]
    for value in parts[1:]:
        out = out + value.astype(jnp.float32)
    return out


def in_place(parts, here):
    parts = jnp.stack(parts)
    return jnp.stack([lax.dynamic_index_in_dim(parts, m ^ here, keepdims=False) for m in range(4)])


def spread(total, here):
    rows = total.shape[0] // 4
    total = total.reshape(4, rows, total.shape[1])
    parts = [lax.dynamic_index_in_dim(total, here ^ m, keepdims=False) for m in range(4)]
    return parts[:1] + [part.astype(jnp.bfloat16) for part in parts[1:]]


def complex_right(value):
    half = value.shape[1] // 2
    return jnp.concatenate([value, jnp.concatenate([-value[:, half:], value[:, :half]], axis=1)], axis=0)


def by_owner(value, nrows):
    return value.reshape(2, 2, 4, nrows, -1).transpose(0, 2, 1, 3, 4).reshape(16 * nrows, -1)


def steps(eigvec, momenta, peram):
    tau = peram[0]
    nrows, nvec = tau.shape[1], tau.shape[3]
    place = lax.axis_index("space")
    quad = place // 2 % 4
    member = place // 8 * 2 + place % 2
    tau = tau.transpose(2, 1, 0, 3).reshape(SPIN, nrows, 2 * nvec)
    sink = gram(eigvec, momenta, 0, tau)
    source = gram(eigvec, momenta, 1)
    sink = around(sink, MEMBER_BITS)
    spins = [lax.dynamic_index_in_dim(tau, member, keepdims=False)] + [part[4 * nrows :] for part in sink[1:]]
    spins = in_place(spins, member)
    source = around(source, MEMBER_BITS)
    spins = around([spins.reshape(4 * nrows, 2 * nvec)] * 4, QUAD_BITS)
    sink = spread(wide_sum([sink[0]] + [part[: 4 * nrows] for part in sink[1:]]), quad)
    source = wide_sum(source)
    source = spread(source, quad)
    second = around([None] + [jnp.concatenate([source[m], sink[m]]) for m in (1, 2, 3)], QUAD_BITS)
    source = wide_sum([source[0]] + [part[:nrows] for part in second[1:]]).astype(jnp.bfloat16)
    sink = wide_sum([sink[0]] + [part[nrows:] for part in second[1:]]).astype(jnp.bfloat16)
    source = lax.ppermute(source, "tm", [(t, 15 - t) for t in range(16)])
    rows = jnp.concatenate(around([sink] * 4, MEMBER_BITS))
    source = in_place(around([source] * 4, QUAD_BITS), quad).reshape(4 * nrows, 2 * nvec)
    spins = in_place(spins, quad).reshape(4, 4, nrows, 2 * nvec).transpose(1, 0, 2, 3)
    mixed = jnp.dot(rows, complex_right(by_owner(spins, nrows)), preferred_element_type=jnp.float32)
    mixed = mixed.astype(jnp.bfloat16).reshape(4, nrows, 2 * nvec)
    third = around([None] + [jnp.concatenate([source, mixed[m]]) for m in (1, 2, 3)], MEMBER_BITS)
    mixed = in_place([mixed[0]] + [part[4 * nrows :] for part in third[1:]], member)
    mixed = mixed.transpose(1, 0, 2).reshape(nrows * SPIN, 2 * nvec)
    source = in_place([source] + [part[: 4 * nrows] for part in third[1:]], member)
    dressed = jnp.dot(mixed, complex_right(by_owner(source, nrows)), preferred_element_type=jnp.float32)
    return dressed.reshape(1, nrows, SPIN, 2, nvec).astype(jnp.bfloat16)


def solution(mesh):
    return jax.shard_map(
        steps,
        mesh=mesh,
        in_specs=(P("tm", None, None, "space", None), P(), P("tm", None, "space", None, None)),
        out_specs=P("tm", "space", None, None, None),
        check_vma=False,
    )
```

```python
import functools
import math

import jax
import jax.numpy as jnp
from jax import lax
from jax.experimental import pallas as pl
from jax.experimental.pallas import tpu as pltpu
from jax.sharding import PartitionSpec as P


LAT = 32
LANES = 128
SPIN = 4
MEMBER_BITS = (0, 1, 8, 9)
QUAD_BITS = (0, 2, 4, 6)


def phase_of(winding):
    octant = (winding & 31) + 4
    quadrant = (octant >> 3) & 3
    angle = ((octant & 7) - 4).astype(jnp.float32) * (2.0 * math.pi / LAT)
    square = angle * angle
    sine = angle * (1 + square * (-1 / 6 + square * (1 / 120 + square * (-1 / 5040 + square * (1 / 362880)))))
    cosine = 1 + square * (-1 / 2 + square * (1 / 24 + square * (-1 / 720 + square * (1 / 40320 - square * (1 / 3628800)))))
    swap = (quadrant & 1) == 1
    cos_out = jnp.where(swap, sine, cosine)
    sin_out = jnp.where(swap, cosine, sine)
    cos_out = jnp.where((quadrant == 1) | (quadrant == 2), -cos_out, cos_out)
    sin_out = jnp.where(quadrant >= 2, -sin_out, sin_out)
    return cos_out, sin_out


def gram_kernel(which, chunks, momenta, vec_ref, spin_ref, keep_ref, *refs):
    send_refs = refs[:3]
    vec_buf, y_ref, left0, left1, right0, right1, acc_ref, sems = refs[3:]
    left = (left0, left1)
    right = (right0, right1)
    _, _, colors, sites, nvec = vec_ref.shape
    depth = sites // chunks
    rows_y = depth // LAT

    def fetch(step):
        return pltpu.make_async_copy(
            vec_ref.at[0, :, :, pl.ds(step * depth, depth), :], vec_buf.at[step], sems.at[step])

    for step in range(chunks):
        fetch(step).start()
    space = lax.axis_index("space")
    index = lax.broadcasted_iota(jnp.int32, (LAT, LANES), 0)
    cos_x, sin_x = phase_of(momenta[which, 0] * index)
    cos_y, sin_y = phase_of(momenta[which, 1] * index + momenta[which, 2] * space)
    y_ref[0] = cos_y
    y_ref[1] = sin_y

    def prepare(step):
        fetch(step).wait()
        for y in range(rows_y):
            at_y = step * rows_y + y
            cos_row = jnp.broadcast_to(y_ref[0, at_y : at_y + 1], (LAT, LANES))
            sin_row = jnp.broadcast_to(y_ref[1, at_y : at_y + 1], (LAT, LANES))
            cosine = cos_x * cos_row - sin_x * sin_row
            sine = sin_x * cos_row + cos_x * sin_row
            cosine = jnp.concatenate([cosine] * (nvec // LANES), axis=1)
            sine = jnp.concatenate([sine] * (nvec // LANES), axis=1)
            for color in range(colors):
                re = vec_buf[step, 0, color, y * LAT : (y + 1) * LAT]
                im = vec_buf[step, 1, color, y * LAT : (y + 1) * LAT]
                re32 = re.astype(jnp.float32)
                im32 = im.astype(jnp.float32)
                at = pl.ds(color * depth + y * LAT, LAT)
                right[step % 2][at, :nvec] = (cosine * re32 + sine * im32).astype(jnp.bfloat16)
                right[step % 2][at, nvec:] = (cosine * im32 - sine * re32).astype(jnp.bfloat16)
                left[step % 2][at, :nvec] = re
                left[step % 2][at, nvec:] = im

    prepare(0)
    for step in range(chunks):
        if step + 1 < chunks:
            prepare(step + 1)
        part = lax.dot_general(left[step % 2][...], right[step % 2][...], (((0,), (0,)), ((), ())),
                               preferred_element_type=jnp.float32)
        if step == 0:
            acc_ref[...] = part
        else:
            acc_ref[...] += part
    rows = nvec // 16
    here = space // 8 * 2 + space % 2
    for member, out_ref in enumerate((keep_ref, *send_refs)):
        target = space ^ MEMBER_BITS[member]
        for quad in range(4):
            owner = (target & 9) | (2 * quad)
            start = pl.multiple_of(owner * rows, 8)
            real = pl.ds(start, rows)
            imag = pl.ds(pl.multiple_of(start + nvec, 8), rows)
            at = pl.ds(quad * rows, rows)
            out_ref[at, :nvec] = (acc_ref[real, :nvec] + acc_ref[imag, nvec:]).astype(out_ref.dtype)
            out_ref[at, nvec:] = (acc_ref[real, nvec:] - acc_ref[imag, :nvec]).astype(out_ref.dtype)
        if spin_ref is not None and member:
            out_ref[pl.ds(4 * rows, rows), :] = spin_ref[here ^ member]


def gram(eigvec, momenta, which, spins=None, chunks=4):
    _, _, colors, sites, nvec = eigvec.shape
    depth = sites // chunks
    rows = nvec // 4
    extra = 0 if spins is None else spins.shape[1]
    outs = [((rows, 2 * nvec), jnp.float32)] + [((rows + extra, 2 * nvec), jnp.bfloat16)] * 3
    vmem = pl.BlockSpec(memory_space=pltpu.VMEM)
    kern = functools.partial(gram_kernel, which, chunks)
    if spins is None:
        body = lambda m, v, *r: kern(m, v, None, *r)
        ins = ()
    else:
        body = kern
        ins = (spins,)
    operand = pltpu.VMEM((colors * depth, 2 * nvec), jnp.bfloat16)
    return pl.pallas_call(
        body,
        in_specs=[pl.BlockSpec(memory_space=pltpu.SMEM), pl.BlockSpec(memory_space=pl.ANY)] + [vmem] * len(ins),
        out_specs=[vmem] * 4,
        scratch_shapes=[
            pltpu.VMEM((chunks, 2, colors, depth, nvec), jnp.bfloat16),
            pltpu.VMEM((2, LAT, LANES), jnp.float32),
            operand, operand, operand, operand,
            pltpu.VMEM((2 * nvec, 2 * nvec), jnp.float32),
            pltpu.SemaphoreType.DMA((chunks,)),
        ],
        out_shape=[jax.ShapeDtypeStruct(shape, kind) for shape, kind in outs],
        compiler_params=pltpu.CompilerParams(vmem_limit_bytes=62 << 20),
        cost_estimate=pl.CostEstimate(flops=8 * nvec * nvec * colors * sites, bytes_accessed=eigvec.size * 2, transcendentals=0),
    )(momenta, eigvec, *ins)


def swap(value, bits):
    return lax.ppermute(value, "space", [(i, i ^ bits) for i in range(16)])


def around(parts, bits):
    return [parts[0]] + [swap(parts[m], bits[m]) for m in (1, 2, 3)]


def wide_sum(parts):
    out = parts[0]
    for value in parts[1:]:
        out = out + value.astype(jnp.float32)
    return out


def in_place(parts, here):
    parts = jnp.stack(parts)
    return jnp.stack([lax.dynamic_index_in_dim(parts, m ^ here, keepdims=False) for m in range(4)])


def spread(total, here):
    rows = total.shape[0] // 4
    total = total.reshape(4, rows, total.shape[1])
    parts = [lax.dynamic_index_in_dim(total, here ^ m, keepdims=False) for m in range(4)]
    return parts[:1] + [part.astype(jnp.bfloat16) for part in parts[1:]]


def complex_right(value):
    half = value.shape[1] // 2
    return jnp.concatenate([value, jnp.concatenate([-value[:, half:], value[:, :half]], axis=1)], axis=0)


def by_owner(value, nrows):
    return value.reshape(2, 2, 4, nrows, -1).transpose(0, 2, 1, 3, 4).reshape(16 * nrows, -1)


def steps(eigvec, momenta, peram):
    tau = peram[0]
    nrows, nvec = tau.shape[1], tau.shape[3]
    place = lax.axis_index("space")
    quad = place // 2 % 4
    member = place // 8 * 2 + place % 2
    tau = tau.transpose(2, 1, 0, 3).reshape(SPIN, nrows, 2 * nvec)
    sink = gram(eigvec, momenta, 0, tau)
    source = gram(eigvec, momenta, 1)
    sink = around(sink, MEMBER_BITS)
    spins = [lax.dynamic_index_in_dim(tau, member, keepdims=False)] + [part[4 * nrows :] for part in sink[1:]]
    spins = in_place(spins, member)
    source = around(source, MEMBER_BITS)
    spins = spins.reshape(4 * nrows, 2 * nvec)
    below, above = swap(spins, 2), swap(spins, 6)
    sink = spread(wide_sum([sink[0]] + [part[: 4 * nrows] for part in sink[1:]]), quad)
    source = wide_sum(source)
    source = spread(source, quad)
    second = around([None] + [jnp.concatenate([source[m], sink[m]]) for m in (1, 2, 3)], QUAD_BITS)
    source = wide_sum([source[0]] + [part[:nrows] for part in second[1:]]).astype(jnp.bfloat16)
    sink = wide_sum([sink[0]] + [part[nrows:] for part in second[1:]]).astype(jnp.bfloat16)
    source = lax.ppermute(source, "tm", [(t, 15 - t) for t in range(16)])
    across = jnp.concatenate([swap(above[: 2 * nrows], 2), swap(below[2 * nrows :], 6)])
    rows = jnp.concatenate([sink, swap(sink, 1)])
    rows = jnp.concatenate([rows, swap(rows, 8)])
    source = in_place(around([source] * 4, QUAD_BITS), quad).reshape(4 * nrows, 2 * nvec)
    spins = in_place([spins, below, across, above], quad).reshape(4, 4, nrows, 2 * nvec).transpose(1, 0, 2, 3)
    mixed = jnp.dot(rows, complex_right(by_owner(spins, nrows)), preferred_element_type=jnp.float32)
    mixed = mixed.astype(jnp.bfloat16).reshape(4, nrows, 2 * nvec)
    third = around([None] + [jnp.concatenate([source, mixed[m]]) for m in (1, 2, 3)], MEMBER_BITS)
    mixed = in_place([mixed[0]] + [part[4 * nrows :] for part in third[1:]], member)
    mixed = mixed.transpose(1, 0, 2).reshape(nrows * SPIN, 2 * nvec)
    source = in_place([source] + [part[: 4 * nrows] for part in third[1:]], member)
    dressed = jnp.dot(mixed, complex_right(by_owner(source, nrows)), preferred_element_type=jnp.float32)
    return dressed.reshape(1, nrows, SPIN, 2, nvec).astype(jnp.bfloat16)


def solution(mesh):
    return jax.shard_map(
        steps,
        mesh=mesh,
        in_specs=(P("tm", None, None, "space", None), P(), P("tm", None, "space", None, None)),
        out_specs=P("tm", "space", None, None, None),
        check_vma=False,
    )
```

```python
import functools
import math

import jax
import jax.numpy as jnp
from jax import lax
from jax.experimental import pallas as pl
from jax.experimental.pallas import tpu as pltpu
from jax.sharding import PartitionSpec as P


LAT = 32
LANES = 128
SPIN = 4
MEMBER_BITS = (0, 1, 8, 9)
QUAD_BITS = (0, 2, 4, 6)


def phase_of(winding):
    octant = (winding & 31) + 4
    quadrant = (octant >> 3) & 3
    angle = ((octant & 7) - 4).astype(jnp.float32) * (2.0 * math.pi / LAT)
    square = angle * angle
    sine = angle * (1 + square * (-1 / 6 + square * (1 / 120 + square * (-1 / 5040 + square * (1 / 362880)))))
    cosine = 1 + square * (-1 / 2 + square * (1 / 24 + square * (-1 / 720 + square * (1 / 40320 - square * (1 / 3628800)))))
    swap = (quadrant & 1) == 1
    cos_out = jnp.where(swap, sine, cosine)
    sin_out = jnp.where(swap, cosine, sine)
    cos_out = jnp.where((quadrant == 1) | (quadrant == 2), -cos_out, cos_out)
    sin_out = jnp.where(quadrant >= 2, -sin_out, sin_out)
    return cos_out, sin_out


def gram_kernel(which, sizes, momenta, vec_ref, spin_ref, keep_ref, *refs):
    send_refs = refs[:3]
    vec_buf, y_ref, right0, right1, acc_ref, sems = refs[3:]
    right = (right0, right1)
    _, parts, colors, _, nvec = vec_ref.shape
    chunks = len(sizes)
    starts = [sum(sizes[:i]) for i in range(chunks)]

    def fetch(step):
        at = pl.ds(starts[step], sizes[step])
        return pltpu.make_async_copy(vec_ref.at[0, :, :, at, :], vec_buf.at[:, :, at, :], sems.at[step])

    for step in range(chunks):
        fetch(step).start()
    space = lax.axis_index("space")
    index = lax.broadcasted_iota(jnp.int32, (LAT, LANES), 0)
    cos_x, sin_x = phase_of(momenta[which, 0] * index)
    cos_y, sin_y = phase_of(momenta[which, 1] * index + momenta[which, 2] * space)
    y_ref[0] = cos_y
    y_ref[1] = sin_y

    def prepare(step):
        fetch(step).wait()
        out = right[step % 2]
        depth = sizes[step]
        half = colors * depth
        for y in range(depth // LAT):
            at_y = starts[step] // LAT + y
            cos_row = jnp.broadcast_to(y_ref[0, at_y : at_y + 1], (LAT, LANES))
            sin_row = jnp.broadcast_to(y_ref[1, at_y : at_y + 1], (LAT, LANES))
            cosine = cos_x * cos_row - sin_x * sin_row
            sine = sin_x * cos_row + cos_x * sin_row
            cosine = jnp.concatenate([cosine] * (nvec // LANES), axis=1)
            sine = jnp.concatenate([sine] * (nvec // LANES), axis=1)
            for color in range(colors):
                re32 = vec_buf[0, color, at_y * LAT : (at_y + 1) * LAT].astype(jnp.float32)
                im32 = vec_buf[1, color, at_y * LAT : (at_y + 1) * LAT].astype(jnp.float32)
                at = color * depth + y * LAT
                real = (cosine * re32 + sine * im32).astype(jnp.bfloat16)
                imag = (cosine * im32 - sine * re32).astype(jnp.bfloat16)
                out[at : at + LAT, :nvec] = real
                out[at : at + LAT, nvec:] = imag
                out[half + at : half + at + LAT, :nvec] = imag
                out[half + at : half + at + LAT, nvec:] = -real

    def multiply(step):
        depth = sizes[step]
        half = colors * depth
        for p in range(parts):
            left = vec_buf[p, :, starts[step] : starts[step] + depth, :].reshape(half, nvec)
            term = lax.dot_general(
                left,
                right[step % 2][p * half : (p + 1) * half, :],
                (((0,), (0,)), ((), ())),
                preferred_element_type=jnp.float32,
            )
            at = pl.ds(p * nvec, nvec)
            acc_ref[at, :] = term if step == 0 else acc_ref[at, :] + term

    prepare(0)
    for step in range(chunks):
        if step + 1 < chunks:
            prepare(step + 1)
        multiply(step)
    rows = nvec // 16
    here = space // 8 * 2 + space % 2
    for member, out_ref in enumerate((keep_ref, *send_refs)):
        target = space ^ MEMBER_BITS[member]
        for quad in range(4):
            owner = (target & 9) | (2 * quad)
            start = pl.multiple_of(owner * rows, 8)
            value = acc_ref[pl.ds(start, rows), :] + acc_ref[pl.ds(pl.multiple_of(start + nvec, 8), rows), :]
            out_ref[pl.ds(quad * rows, rows), :] = value.astype(out_ref.dtype)
        if spin_ref is not None and member:
            out_ref[pl.ds(4 * rows, rows), :] = spin_ref[here ^ member]


def gram(eigvec, momenta, which, spins=None, sizes=(128, 256, 256, 256, 128)):
    _, _, colors, sites, nvec = eigvec.shape
    depth = max(sizes)
    chunks = len(sizes)
    rows = nvec // 4
    extra = 0 if spins is None else spins.shape[1]
    outs = [((rows, 2 * nvec), jnp.float32)] + [((rows + extra, 2 * nvec), jnp.bfloat16)] * 3
    vmem = pl.BlockSpec(memory_space=pltpu.VMEM)
    kern = functools.partial(gram_kernel, which, sizes)
    if spins is None:
        body = lambda m, v, *r: kern(m, v, None, *r)
        ins = ()
    else:
        body = kern
        ins = (spins,)
    operand = pltpu.VMEM((2 * colors * depth, 2 * nvec), jnp.bfloat16)
    return pl.pallas_call(
        body,
        in_specs=[pl.BlockSpec(memory_space=pltpu.SMEM), pl.BlockSpec(memory_space=pltpu.HBM)] + [vmem] * len(ins),
        out_specs=[vmem] * 4,
        scratch_shapes=[
            pltpu.VMEM((2, colors, sites, nvec), jnp.bfloat16),
            pltpu.VMEM((2, LAT, LANES), jnp.float32),
            operand, operand,
            pltpu.VMEM((2 * nvec, 2 * nvec), jnp.float32),
            pltpu.SemaphoreType.DMA((chunks,)),
        ],
        out_shape=[jax.ShapeDtypeStruct(shape, kind) for shape, kind in outs],
        compiler_params=pltpu.CompilerParams(vmem_limit_bytes=51 << 20),
        cost_estimate=pl.CostEstimate(flops=8 * nvec * nvec * colors * sites, bytes_accessed=eigvec.size * 2, transcendentals=0),
    )(momenta, eigvec, *ins)


def swap(value, bits):
    return lax.ppermute(value, "space", [(i, i ^ bits) for i in range(16)])


def around(parts, bits):
    return [parts[0]] + [swap(parts[m], bits[m]) for m in (1, 2, 3)]


def wide_sum(parts):
    out = parts[0]
    for value in parts[1:]:
        out = out + value.astype(jnp.float32)
    return out


def in_place(parts, here):
    parts = jnp.stack(parts)
    return jnp.stack([lax.dynamic_index_in_dim(parts, m ^ here, keepdims=False) for m in range(4)])


def spread(total, here):
    rows = total.shape[0] // 4
    total = total.reshape(4, rows, total.shape[1])
    parts = [lax.dynamic_index_in_dim(total, here ^ m, keepdims=False) for m in range(4)]
    return parts[:1] + [part.astype(jnp.bfloat16) for part in parts[1:]]


def complex_right(value):
    half = value.shape[1] // 2
    return jnp.concatenate([value, jnp.concatenate([-value[:, half:], value[:, :half]], axis=1)], axis=0)


def by_owner(value, nrows):
    return value.reshape(2, 2, 4, nrows, -1).transpose(0, 2, 1, 3, 4).reshape(16 * nrows, -1)


def steps(eigvec, momenta, peram):
    tau = peram[0]
    nrows, nvec = tau.shape[1], tau.shape[3]
    place = lax.axis_index("space")
    quad = place // 2 % 4
    member = place // 8 * 2 + place % 2
    tau = tau.transpose(2, 1, 0, 3).reshape(SPIN, nrows, 2 * nvec)
    sink = gram(eigvec, momenta, 0, tau)
    source = gram(eigvec, momenta, 1)
    sink = around(sink, MEMBER_BITS)
    spins = [lax.dynamic_index_in_dim(tau, member, keepdims=False)] + [part[4 * nrows :] for part in sink[1:]]
    spins = in_place(spins, member)
    source = around(source, MEMBER_BITS)
    spins = spins.reshape(4 * nrows, 2 * nvec)
    below, above = swap(spins, 2), swap(spins, 6)
    sink = spread(wide_sum([sink[0]] + [part[: 4 * nrows] for part in sink[1:]]), quad)
    source = wide_sum(source)
    source = spread(source, quad)
    second = around([None] + [jnp.concatenate([source[m], sink[m]]) for m in (1, 2, 3)], QUAD_BITS)
    source = wide_sum([source[0]] + [part[:nrows] for part in second[1:]]).astype(jnp.bfloat16)
    sink = wide_sum([sink[0]] + [part[nrows:] for part in second[1:]]).astype(jnp.bfloat16)
    source = lax.ppermute(source, "tm", [(t, 15 - t) for t in range(16)])
    across = jnp.concatenate([swap(above[: 2 * nrows], 2), swap(below[2 * nrows :], 6)])
    rows = jnp.concatenate([sink, swap(sink, 1)])
    rows = jnp.concatenate([rows, swap(rows, 8)])
    source = in_place(around([source] * 4, QUAD_BITS), quad).reshape(4 * nrows, 2 * nvec)
    spins = in_place([spins, below, across, above], quad).reshape(4, 4, nrows, 2 * nvec).transpose(1, 0, 2, 3)
    mixed = jnp.dot(rows, complex_right(by_owner(spins, nrows)), preferred_element_type=jnp.float32)
    mixed = mixed.astype(jnp.bfloat16).reshape(4, nrows, 2 * nvec)
    third = around([None] + [jnp.concatenate([source, mixed[m]]) for m in (1, 2, 3)], MEMBER_BITS)
    mixed = in_place([mixed[0]] + [part[4 * nrows :] for part in third[1:]], member)
    mixed = mixed.transpose(1, 0, 2).reshape(nrows * SPIN, 2 * nvec)
    source = in_place([source] + [part[: 4 * nrows] for part in third[1:]], member)
    dressed = jnp.dot(mixed, complex_right(by_owner(source, nrows)), preferred_element_type=jnp.float32)
    dressed = lax.optimization_barrier(dressed.astype(jnp.bfloat16))
    return dressed.reshape(1, nrows, SPIN, 2, nvec)


def solution(mesh):
    return jax.shard_map(
        steps,
        mesh=mesh,
        in_specs=(P("tm", None, None, "space", None), P(), P("tm", None, "space", None, None)),
        out_specs=P("tm", "space", None, None, None),
        check_vma=False,
    )
```

```python
import functools
import math

import jax
import jax.numpy as jnp
from jax import lax
from jax.experimental import pallas as pl
from jax.experimental.pallas import tpu as pltpu
from jax.sharding import PartitionSpec as P


LAT = 32
LANES = 128
SPIN = 4
MEMBER_BITS = (0, 1, 8, 9)


def phase_of(winding):
    octant = (winding & 31) + 4
    quadrant = (octant >> 3) & 3
    angle = ((octant & 7) - 4).astype(jnp.float32) * (2.0 * math.pi / LAT)
    square = angle * angle
    sine = angle * (1 + square * (-1 / 6 + square * (1 / 120 + square * (-1 / 5040 + square * (1 / 362880)))))
    cosine = 1 + square * (-1 / 2 + square * (1 / 24 + square * (-1 / 720 + square * (1 / 40320 - square * (1 / 3628800)))))
    swap = (quadrant & 1) == 1
    cos_out = jnp.where(swap, sine, cosine)
    sin_out = jnp.where(swap, cosine, sine)
    cos_out = jnp.where((quadrant == 1) | (quadrant == 2), -cos_out, cos_out)
    sin_out = jnp.where(quadrant >= 2, -sin_out, sin_out)
    return cos_out, sin_out


def gram_kernel(which, sizes, momenta, vec_ref, spin_ref, keep_ref, *refs):
    send_refs = refs[:3]
    vec_buf, y_ref, right0, right1, acc_ref, sems = refs[3:]
    right = (right0, right1)
    _, parts, colors, _, nvec = vec_ref.shape
    chunks = len(sizes)
    starts = [sum(sizes[:i]) for i in range(chunks)]

    def fetch(step):
        at = pl.ds(starts[step], sizes[step])
        return pltpu.make_async_copy(vec_ref.at[0, :, :, at, :], vec_buf.at[:, :, at, :], sems.at[step])

    for step in range(chunks):
        fetch(step).start()
    space = lax.axis_index("space")
    index = lax.broadcasted_iota(jnp.int32, (LAT, LANES), 0)
    cos_x, sin_x = phase_of(momenta[which, 0] * index)
    cos_y, sin_y = phase_of(momenta[which, 1] * index + momenta[which, 2] * space)
    y_ref[0] = cos_y
    y_ref[1] = sin_y

    def prepare(step):
        fetch(step).wait()
        out = right[step % 2]
        depth = sizes[step]
        half = colors * depth
        for y in range(depth // LAT):
            at_y = starts[step] // LAT + y
            cos_row = jnp.broadcast_to(y_ref[0, at_y : at_y + 1], (LAT, LANES))
            sin_row = jnp.broadcast_to(y_ref[1, at_y : at_y + 1], (LAT, LANES))
            cosine = cos_x * cos_row - sin_x * sin_row
            sine = sin_x * cos_row + cos_x * sin_row
            cosine = jnp.concatenate([cosine] * (nvec // LANES), axis=1)
            sine = jnp.concatenate([sine] * (nvec // LANES), axis=1)
            for color in range(colors):
                re32 = vec_buf[0, color, at_y * LAT : (at_y + 1) * LAT].astype(jnp.float32)
                im32 = vec_buf[1, color, at_y * LAT : (at_y + 1) * LAT].astype(jnp.float32)
                at = color * depth + y * LAT
                real = (cosine * re32 + sine * im32).astype(jnp.bfloat16)
                imag = (cosine * im32 - sine * re32).astype(jnp.bfloat16)
                out[at : at + LAT, :nvec] = real
                out[at : at + LAT, nvec:] = imag
                out[half + at : half + at + LAT, :nvec] = imag
                out[half + at : half + at + LAT, nvec:] = -real

    def multiply(step):
        depth = sizes[step]
        half = colors * depth
        if half % 256:
            left = vec_buf[:, :, starts[step] : starts[step] + depth, :].reshape(parts * half, nvec)
            spans = [(left, 0, parts * half, step % parts)]
        else:
            spans = [
                (vec_buf[p, :, starts[step] : starts[step] + depth, :].reshape(half, nvec), p * half, half, p)
                for p in range(parts)
            ]
        for left, start, length, slot in spans:
            term = lax.dot_general(
                left,
                right[step % 2][start : start + length, :],
                (((0,), (0,)), ((), ())),
                preferred_element_type=jnp.float32,
            )
            at = pl.ds(slot * nvec, nvec)
            acc_ref[at, :] = acc_ref[at, :] + term if slot in filled else term
            filled.add(slot)

    filled = set()
    prepare(0)
    for step in range(chunks):
        if step + 1 < chunks:
            prepare(step + 1)
        multiply(step)
    rows = nvec // 16
    here = space // 8 * 2 + space % 2
    for member, out_ref in enumerate((keep_ref, *send_refs)):
        target = space ^ MEMBER_BITS[member]
        for quad in range(4):
            owner = (target & 9) | (2 * quad)
            start = pl.multiple_of(owner * rows, 8)
            value = acc_ref[pl.ds(start, rows), :] + acc_ref[pl.ds(pl.multiple_of(start + nvec, 8), rows), :]
            out_ref[pl.ds(quad * rows, rows), :] = value.astype(out_ref.dtype)
        if spin_ref is not None and member:
            out_ref[pl.ds(4 * rows, rows), :] = spin_ref[here ^ member]


def gram(eigvec, momenta, which, spins=None, sizes=(128, 128, 256, 256, 256)):
    _, _, colors, sites, nvec = eigvec.shape
    depth = max(sizes)
    chunks = len(sizes)
    rows = nvec // 4
    extra = 0 if spins is None else spins.shape[1]
    outs = [((rows, 2 * nvec), jnp.float32)] + [((rows + extra, 2 * nvec), jnp.bfloat16)] * 3
    vmem = pl.BlockSpec(memory_space=pltpu.VMEM)
    kern = functools.partial(gram_kernel, which, sizes)
    if spins is None:
        body = lambda m, v, *r: kern(m, v, None, *r)
        ins = ()
    else:
        body = kern
        ins = (spins,)
    operand = pltpu.VMEM((2 * colors * depth, 2 * nvec), jnp.bfloat16)
    return pl.pallas_call(
        body,
        in_specs=[pl.BlockSpec(memory_space=pltpu.SMEM), pl.BlockSpec(memory_space=pltpu.HBM)] + [vmem] * len(ins),
        out_specs=[vmem] * 4,
        scratch_shapes=[
            pltpu.VMEM((2, colors, sites, nvec), jnp.bfloat16),
            pltpu.VMEM((2, LAT, LANES), jnp.float32),
            operand, operand,
            pltpu.VMEM((2 * nvec, 2 * nvec), jnp.float32),
            pltpu.SemaphoreType.DMA((chunks,)),
        ],
        out_shape=[jax.ShapeDtypeStruct(shape, kind) for shape, kind in outs],
        compiler_params=pltpu.CompilerParams(vmem_limit_bytes=51 << 20),
        cost_estimate=pl.CostEstimate(flops=8 * nvec * nvec * colors * sites, bytes_accessed=eigvec.size * 2, transcendentals=0),
    )(pltpu.with_memory_space_constraint(momenta, pltpu.HBM), eigvec, *ins)


def swap(value, bits):
    return lax.ppermute(value, "space", [(i, i ^ bits) for i in range(16)])


def around(parts, bits):
    return [parts[0]] + [swap(parts[m], bits[m]) for m in (1, 2, 3)]


def wide_sum(parts):
    out = parts[0]
    for value in parts[1:]:
        out = out + value.astype(jnp.float32)
    return out


def in_place(parts, here):
    parts = jnp.stack(parts)
    return jnp.stack([lax.dynamic_index_in_dim(parts, m ^ here, keepdims=False) for m in range(4)])


def spread(total, here):
    rows = total.shape[0] // 4
    total = total.reshape(4, rows, total.shape[1])
    return [lax.dynamic_index_in_dim(total, here ^ m, keepdims=False) for m in range(4)]


def complex_right(value):
    half = value.shape[1] // 2
    return jnp.concatenate([value, jnp.concatenate([-value[:, half:], value[:, :half]], axis=1)], axis=0)


def by_owner(value, nrows):
    return value.reshape(2, 2, 4, nrows, -1).transpose(0, 2, 1, 3, 4).reshape(16 * nrows, -1)


def steps(eigvec, momenta, peram):
    tau = peram[0]
    nrows, nvec = tau.shape[1], tau.shape[3]
    place = lax.axis_index("space")
    quad = place // 2 % 4
    member = place // 8 * 2 + place % 2
    tau = tau.transpose(2, 1, 0, 3).reshape(SPIN, nrows, 2 * nvec)
    sink = gram(eigvec, momenta, 0, tau)
    source = gram(eigvec, momenta, 1)
    sink = around(sink, MEMBER_BITS)
    spins = [lax.dynamic_index_in_dim(tau, member, keepdims=False)] + [part[4 * nrows :] for part in sink[1:]]
    spins = in_place(spins, member)
    source = around(source, MEMBER_BITS)
    spins = spins.reshape(4 * nrows, 2 * nvec)
    below, above = swap(spins, 2), swap(spins, 6)
    sink = spread(wide_sum([sink[0]] + [part[: 4 * nrows] for part in sink[1:]]), quad)
    source = wide_sum(source)
    source = spread(source, quad)
    left = swap(source[2].astype(jnp.bfloat16), 2)
    right = swap(sink[2].astype(jnp.bfloat16), 6)
    left = wide_sum([source[3], left])
    right = wide_sum([sink[1], right])
    to_left = jnp.concatenate([source[1], right]).astype(jnp.bfloat16)
    to_right = jnp.concatenate([left, sink[3]]).astype(jnp.bfloat16)
    second = [swap(to_left, 2), swap(to_right, 6)]
    source = wide_sum([source[0]] + [part[:nrows] for part in second]).astype(jnp.bfloat16)
    sink = wide_sum([sink[0]] + [part[nrows:] for part in second]).astype(jnp.bfloat16)
    source = lax.ppermute(source, "tm", [(t, 15 - t) for t in range(16)])
    across = jnp.concatenate([swap(above[: 2 * nrows], 2), swap(below[2 * nrows :], 6)])
    rows = jnp.concatenate([sink, swap(sink, 1)])
    rows = jnp.concatenate([rows, swap(rows, 8)])
    left, right = swap(source, 2), swap(source, 6)
    opposite = jnp.concatenate([swap(right[:16], 2), swap(left[16:], 6)])
    source = in_place([source, left, opposite, right], quad).reshape(4 * nrows, 2 * nvec)
    spins = in_place([spins, below, across, above], quad).reshape(4, 4, nrows, 2 * nvec).transpose(1, 0, 2, 3)
    mixed = jnp.dot(rows, complex_right(by_owner(spins, nrows)), preferred_element_type=jnp.float32)
    mixed = mixed.astype(jnp.bfloat16).reshape(4, nrows, 2 * nvec)
    third = around([None] + [jnp.concatenate([source, mixed[m]]) for m in (1, 2, 3)], MEMBER_BITS)
    mixed = in_place([mixed[0]] + [part[4 * nrows :] for part in third[1:]], member)
    mixed = mixed.transpose(1, 0, 2).reshape(nrows * SPIN, 2 * nvec)
    source = in_place([source] + [part[: 4 * nrows] for part in third[1:]], member)
    dressed = jnp.dot(mixed, complex_right(by_owner(source, nrows)), preferred_element_type=jnp.float32)
    dressed = lax.optimization_barrier(dressed.astype(jnp.bfloat16))
    return dressed.reshape(1, nrows, SPIN, 2, nvec)


def solution(mesh):
    return jax.shard_map(
        steps,
        mesh=mesh,
        in_specs=(P("tm", None, None, "space", None), P(), P("tm", None, "space", None, None)),
        out_specs=P("tm", "space", None, None, None),
        check_vma=False,
    )
```

```python
import functools
import math

import jax
import jax.numpy as jnp
from jax import lax
from jax.experimental import pallas as pl
from jax.experimental.pallas import tpu as pltpu
from jax.sharding import PartitionSpec as P


LAT = 32
LANES = 128
SPIN = 4
GRANT = 32
MEMBER_BITS = (0, 1, 8, 9)
QUAD_BITS = (0, 2, 4, 6)


def phase_of(winding):
    octant = (winding & 31) + 4
    quadrant = (octant >> 3) & 3
    angle = ((octant & 7) - 4).astype(jnp.float32) * (2.0 * math.pi / LAT)
    square = angle * angle
    sine = angle * (1 + square * (-1 / 6 + square * (1 / 120 + square * (-1 / 5040 + square * (1 / 362880)))))
    cosine = 1 + square * (-1 / 2 + square * (1 / 24 + square * (-1 / 720 + square * (1 / 40320 - square * (1 / 3628800)))))
    swap = (quadrant & 1) == 1
    cos_out = jnp.where(swap, sine, cosine)
    sin_out = jnp.where(swap, cosine, sine)
    cos_out = jnp.where((quadrant == 1) | (quadrant == 2), -cos_out, cos_out)
    sin_out = jnp.where(quadrant >= 2, -sin_out, sin_out)
    return cos_out, sin_out


def gram_kernel(which, sizes, loads, momenta, vec_ref, *refs):
    if loads:
        spin_ref, keep_ref, *send_refs, vec_buf = refs[:6]
        y_ref, right0, right1, acc_ref, sems = refs[6:]
    else:
        spin_ref, vec_buf = None, vec_ref
        keep_ref, *send_refs = refs[:4]
        y_ref, right0, right1, acc_ref = refs[4:]
    right = (right0, right1)
    _, parts, colors, _, nvec = vec_ref.shape
    chunks = len(sizes)
    starts = [sum(sizes[:i]) for i in range(chunks)]

    def fetch(step):
        at = pl.ds(starts[step], sizes[step])
        return pltpu.make_async_copy(vec_ref.at[0, :, :, at, :], vec_buf.at[0, :, :, at, :], sems.at[step])

    if loads:
        for step in range(chunks):
            fetch(step).start()
    space = lax.axis_index("space")
    index = lax.broadcasted_iota(jnp.int32, (LAT, LANES), 0)
    cos_x, sin_x = phase_of(momenta[which, 0] * index)
    cos_y, sin_y = phase_of(momenta[which, 1] * index + momenta[which, 2] * space)
    y_ref[0] = cos_y
    y_ref[1] = sin_y

    def prepare(step):
        if loads:
            fetch(step).wait()
        out = right[step % 2]
        depth = sizes[step]
        half = colors * depth
        for y in range(depth // LAT):
            at_y = starts[step] // LAT + y
            cos_row = jnp.broadcast_to(y_ref[0, at_y : at_y + 1], (LAT, LANES))
            sin_row = jnp.broadcast_to(y_ref[1, at_y : at_y + 1], (LAT, LANES))
            cosine = cos_x * cos_row - sin_x * sin_row
            sine = sin_x * cos_row + cos_x * sin_row
            cosine = jnp.concatenate([cosine] * (nvec // LANES), axis=1)
            sine = jnp.concatenate([sine] * (nvec // LANES), axis=1)
            for color in range(colors):
                re32 = vec_buf[0, 0, color, at_y * LAT : (at_y + 1) * LAT].astype(jnp.float32)
                im32 = vec_buf[0, 1, color, at_y * LAT : (at_y + 1) * LAT].astype(jnp.float32)
                at = color * depth + y * LAT
                real = (cosine * re32 + sine * im32).astype(jnp.bfloat16)
                imag = (cosine * im32 - sine * re32).astype(jnp.bfloat16)
                out[at : at + LAT, :nvec] = real
                out[at : at + LAT, nvec:] = imag
                out[half + at : half + at + LAT, :nvec] = imag
                out[half + at : half + at + LAT, nvec:] = -real

    def multiply(step):
        depth = sizes[step]
        half = colors * depth
        if half % 256:
            left = vec_buf[0, :, :, starts[step] : starts[step] + depth, :].reshape(parts * half, nvec)
            spans = [(left, 0, parts * half, step % parts)]
        else:
            spans = [
                (vec_buf[0, p, :, starts[step] : starts[step] + depth, :].reshape(half, nvec), p * half, half, p)
                for p in range(parts)
            ]
        for left, start, length, slot in spans:
            term = lax.dot_general(
                left,
                right[step % 2][start : start + length, :],
                (((0,), (0,)), ((), ())),
                preferred_element_type=jnp.float32,
            )
            at = pl.ds(slot * nvec, nvec)
            acc_ref[at, :] = acc_ref[at, :] + term if slot in filled else term
            filled.add(slot)

    filled = set()
    prepare(0)
    for step in range(chunks):
        if step + 1 < chunks:
            prepare(step + 1)
        multiply(step)
    rows = nvec // 16
    here = space // 8 * 2 + space % 2
    for member, out_ref in enumerate((keep_ref, *send_refs)):
        target = space ^ MEMBER_BITS[member]
        for quad in range(4):
            owner = (target & 9) | (2 * quad)
            start = pl.multiple_of(owner * rows, 8)
            value = acc_ref[pl.ds(start, rows), :] + acc_ref[pl.ds(pl.multiple_of(start + nvec, 8), rows), :]
            out_ref[pl.ds(quad * rows, rows), :] = value.astype(out_ref.dtype)
        if spin_ref is not None and member:
            out_ref[pl.ds(4 * rows, rows), :] = spin_ref[here ^ member]


def gram(eigvec, momenta, which, spins=None, sizes=(128, 128, 256, 256, 256)):
    _, _, colors, sites, nvec = eigvec.shape
    depth = max(sizes)
    rows = nvec // 4
    loads = spins is not None
    extra = spins.shape[1] if loads else 0
    outs = [((rows, 2 * nvec), jnp.float32)] + [((rows + extra, 2 * nvec), jnp.bfloat16)] * 3
    vmem = pl.BlockSpec(memory_space=pltpu.VMEM)
    operand = pltpu.VMEM((2 * colors * depth, 2 * nvec), jnp.bfloat16)
    scratch = [
        pltpu.VMEM((2, LAT, LANES), jnp.float32),
        operand,
        operand,
        pltpu.VMEM((2 * nvec, 2 * nvec), jnp.float32),
    ]
    args = [pltpu.with_memory_space_constraint(momenta, pltpu.HBM), eigvec]
    specs = [pl.BlockSpec(memory_space=pltpu.SMEM), vmem]
    if loads:
        args = [args[0], pltpu.with_memory_space_constraint(eigvec, pltpu.HBM), spins]
        specs = [specs[0], pl.BlockSpec(memory_space=pltpu.HBM), vmem]
        outs.append((eigvec.shape, eigvec.dtype))
        scratch.append(pltpu.SemaphoreType.DMA((len(sizes),)))
    return pl.pallas_call(
        functools.partial(gram_kernel, which, sizes, loads),
        in_specs=specs,
        out_specs=[vmem] * len(outs),
        scratch_shapes=scratch,
        out_shape=[jax.ShapeDtypeStruct(shape, kind) for shape, kind in outs],
        compiler_params=pltpu.CompilerParams(vmem_limit_bytes=GRANT << 20),
        cost_estimate=pl.CostEstimate(
            flops=8 * nvec * nvec * colors * sites, bytes_accessed=eigvec.size * 2, transcendentals=0
        ),
    )(*args)


def swap(value, bits):
    return lax.ppermute(value, "space", [(i, i ^ bits) for i in range(16)])


def around(parts, bits):
    return [parts[0]] + [swap(parts[m], bits[m]) for m in (1, 2, 3)]


def wide_sum(parts):
    out = parts[0]
    for value in parts[1:]:
        out = out + value.astype(jnp.float32)
    return out


def in_place(parts, here):
    parts = jnp.stack(parts)
    return jnp.stack([lax.dynamic_index_in_dim(parts, m ^ here, keepdims=False) for m in range(4)])


def spread(total, here):
    rows = total.shape[0] // 4
    total = total.reshape(4, rows, total.shape[1])
    parts = [lax.dynamic_index_in_dim(total, here ^ m, keepdims=False) for m in range(4)]
    return parts[:1] + [part.astype(jnp.bfloat16) for part in parts[1:]]


def complex_right(value):
    half = value.shape[1] // 2
    return jnp.concatenate([value, jnp.concatenate([-value[:, half:], value[:, :half]], axis=1)], axis=0)


def by_owner(value, nrows):
    return value.reshape(2, 2, 4, nrows, -1).transpose(0, 2, 1, 3, 4).reshape(16 * nrows, -1)


def steps(eigvec, momenta, peram):
    tau = peram[0]
    nrows, nvec = tau.shape[1], tau.shape[3]
    place = lax.axis_index("space")
    quad = place // 2 % 4
    member = place // 8 * 2 + place % 2
    tau = tau.transpose(2, 1, 0, 3).reshape(SPIN, nrows, 2 * nvec)
    *sink, vectors = gram(eigvec, momenta, 0, tau)
    source = gram(vectors, momenta, 1)
    sink = around(sink, MEMBER_BITS)
    spins = [lax.dynamic_index_in_dim(tau, member, keepdims=False)] + [part[4 * nrows :] for part in sink[1:]]
    spins = in_place(spins, member)
    source = around(source, MEMBER_BITS)
    spins = spins.reshape(4 * nrows, 2 * nvec)
    below, above = swap(spins, 2), swap(spins, 6)
    sink = spread(wide_sum([sink[0]] + [part[: 4 * nrows] for part in sink[1:]]), quad)
    source = wide_sum(source)
    source = spread(source, quad)
    second = around([None] + [jnp.concatenate([source[m], sink[m]]) for m in (1, 2, 3)], QUAD_BITS)
    source = wide_sum([source[0]] + [part[:nrows] for part in second[1:]]).astype(jnp.bfloat16)
    sink = wide_sum([sink[0]] + [part[nrows:] for part in second[1:]]).astype(jnp.bfloat16)
    source = lax.ppermute(source, "tm", [(t, 15 - t) for t in range(16)])
    across = jnp.concatenate([swap(above[: 2 * nrows], 2), swap(below[2 * nrows :], 6)])
    rows = jnp.concatenate([sink, swap(sink, 1)])
    rows = jnp.concatenate([rows, swap(rows, 8)])
    source = around([source] * 4, QUAD_BITS)
    source = in_place(source, quad).reshape(4 * nrows, 2 * nvec)
    spins = in_place([spins, below, across, above], quad).reshape(4, 4, nrows, 2 * nvec).transpose(1, 0, 2, 3)
    mixed = jnp.dot(rows, complex_right(by_owner(spins, nrows)), preferred_element_type=jnp.float32)
    mixed = mixed.astype(jnp.bfloat16).reshape(4, nrows, 2 * nvec)
    third = around([None] + [jnp.concatenate([source, mixed[m]]) for m in (1, 2, 3)], MEMBER_BITS)
    mixed = in_place([mixed[0]] + [part[4 * nrows :] for part in third[1:]], member)
    mixed = mixed.transpose(1, 0, 2).reshape(nrows * SPIN, 2 * nvec)
    source = in_place([source] + [part[: 4 * nrows] for part in third[1:]], member)
    dressed = jnp.dot(mixed, complex_right(by_owner(source, nrows)), preferred_element_type=jnp.float32)
    dressed = lax.optimization_barrier(dressed.astype(jnp.bfloat16))
    return dressed.reshape(1, nrows, SPIN, 2, nvec)


def solution(mesh):
    return jax.shard_map(
        steps,
        mesh=mesh,
        in_specs=(P("tm", None, None, "space", None), P(), P("tm", None, "space", None, None)),
        out_specs=P("tm", "space", None, None, None),
        check_vma=False,
    )
```
